1024 devices in a mesh: grp: 16 (over x_hi, y), dev: 64 (over z, x_lo, core).
Axes of the slice: x: 4 (x_hi: 2, x_lo: 2; x = x_hi * 2 + x_lo), y: 8, z: 16, core: 2. Of those that a mesh axis runs over, the one named last changes fastest.
Arguments:
- state: float32 [2, 8, 4194304], P(None, None, ('grp', 'dev')), may hold values from -6 to 6
- gates: float32 [2, 4, 2, 128, 128], replicated, may hold values from -0.375 to 0.375
- local_perm: int32 [2, 12], replicated, may hold values from 0 to 11, each once within a row
Outputs:
- final_state: float32 [2, 8, 4194304], P(None, None, ('grp', 'dev'))
The draws below stay inside these ranges and needn't reach their ends.
Inputs may be any that keep to these rules, and one draw needn't show every extreme that they name: Each row of local_perm names each of the 12 local qubits once.
All inputs are finite; a program needn't handle non-finite values.
Results may differ from the reference program's by a relative error of at most 0.0001.
Values sent between devices are 32-bit elements; how exact they have to be, the bound alone decides.
No kernel may reach another device: no remote copies, remote signals or barrier semaphores. Data moves between devices by JAX's collectives and lax.ppermute only.
A program may use at most 32 MiB of HBM per device.

```python
import jax
import jax.numpy as jnp
from jax import lax

GATE_DIM = 128
LOCAL_QUBITS = 12
TRAJ = 8
CYCLES = 2
AMPS = 4194304
N_GRP = 16
N_DEV = 64


def shard_levels(stream_key, shape, shards, least, high):
    def one(position, shards_of):
        heights = jax.random.uniform(jax.random.fold_in(jax.random.fold_in(stream_key, 6), position), (shards_of,), jnp.float32, least / len(shards), high / len(shards))
        return jnp.repeat(jnp.exp(heights), shape[position] // shards_of).reshape((-1,) + (1,) * (len(shape) - position - 1))

    factor_of = one(*shards[0])
    for cut in shards[1:]:
        factor_of = factor_of * one(*cut)
    return factor_of


def bell_draw(rng, dims, spread, reach, shards=(), kind=jnp.bfloat16):
    entries = spread * jax.random.normal(rng, dims, jnp.float32)
    if shards:
        entries = entries * shard_levels(rng, dims, shards, -0.22, 0.18)
    return jnp.clip(entries, -reach, reach).astype(kind)


def setup_inputs(seed: int = 0) -> dict:
    streams_of = jax.random.split(jax.random.key(seed), 4)
    return {
        "state": bell_draw(streams_of[0], (2, TRAJ, AMPS), 1.0, 6.0, ((2, 1024),), jnp.float32),
        "gates": bell_draw(streams_of[1], (CYCLES, 4, 2, GATE_DIM, GATE_DIM), (2 * GATE_DIM) ** -0.5, 0.375, (), jnp.float32),
        "local_perm": jax.vmap(lambda own: jax.random.permutation(own, LOCAL_QUBITS))(jax.random.split(streams_of[2], CYCLES)).reshape((CYCLES, LOCAL_QUBITS)).astype(jnp.int32),
    }


def source_index(perm_row, nbits):
    positions = jnp.arange(2 ** nbits, dtype=jnp.int32)
    shifts = jnp.arange(nbits, dtype=jnp.int32)
    bits = (positions[:, None] >> shifts[None, :]) & 1
    return jnp.sum(bits << perm_row.astype(jnp.int32)[None, :], axis=1).astype(jnp.int32)


def complex_apply(real_part, imag_part, gate, form):
    high = lax.Precision.HIGHEST
    gate_re = gate[0]
    gate_im = gate[1]
    out_re = jnp.einsum(form, real_part, gate_re, precision=high) - jnp.einsum(form, imag_part, gate_im, precision=high)
    out_im = jnp.einsum(form, real_part, gate_im, precision=high) + jnp.einsum(form, imag_part, gate_re, precision=high)
    return jnp.stack([out_re, out_im])


def gate_low(amps, gate):
    shape = amps.shape
    blocks = amps.reshape(2, shape[1], -1, GATE_DIM)
    return complex_apply(blocks[0], blocks[1], gate, "bmk,ik->bmi").reshape(shape)


def gate_high(amps, gate):
    shape = amps.shape
    blocks = amps.reshape(2, shape[1], shape[2], GATE_DIM, -1)
    return complex_apply(blocks[0], blocks[1], gate, "bgkm,ik->bgim").reshape(shape)


def reference(state, gates, local_perm):
    grp_bits = N_GRP.bit_length() - 1
    dev_amps = 2 ** LOCAL_QUBITS
    amps = state.reshape(2, TRAJ, N_GRP * N_DEV, dev_amps)
    for cycle in range(CYCLES):
        source = source_index(local_perm[cycle], LOCAL_QUBITS)
        amps = jnp.take(amps, source, axis=3)
        amps = gate_low(amps, gates[cycle, 0])
        amps = gate_high(amps, gates[cycle, 1])
        which = cycle % grp_bits
        split = amps.reshape(2, TRAJ, N_GRP >> (which + 1), 2, 1 << which, N_DEV, 2, dev_amps // 2)
        amps = jnp.swapaxes(split, 3, 6).reshape(2, TRAJ, N_GRP * N_DEV, dev_amps)
        amps = gate_low(amps, gates[cycle, 2])
        split = amps.reshape(2, TRAJ, N_GRP, N_DEV, N_DEV, dev_amps // N_DEV)
        amps = jnp.swapaxes(split, 3, 4).reshape(2, TRAJ, N_GRP * N_DEV, dev_amps)
        amps = gate_high(amps, gates[cycle, 3])
    return amps.reshape(2, TRAJ, -1)
```

```python
import functools

import jax
import jax.numpy as jnp
from jax import lax
from jax.experimental import pallas as pl
from jax.experimental.pallas import tpu as pltpu
from jax.sharding import PartitionSpec as P

CYCLES = 2
LANE_BITS = 7
TILE_BITS = 5
TILES = 1 << TILE_BITS
SUBLANES = 8
LANES = 1 << LANE_BITS
WIDE = 2 * LANES


def lane_iota(shape):
    return lax.broadcasted_iota(jnp.int32, shape, len(shape) - 1)


def sublane_iota(shape):
    return lax.broadcasted_iota(jnp.int32, shape, len(shape) - 2)


def halves(array):
    high = array.astype(jnp.bfloat16)
    return high, (array - high.astype(jnp.float32)).astype(jnp.bfloat16)


def product(left, right, contract):
    left_high, left_low = halves(left)
    right_high, right_low = halves(right)
    dims = (contract, ((), ()))
    dot = functools.partial(lax.dot_general, dimension_numbers=dims, preferred_element_type=jnp.float32)
    return dot(left_high, right_high) + (dot(left_high, right_low) + dot(left_low, right_high))


def swap_sublane_lane(tiles, sublane_bit, lane_bit):
    step, hop = 1 << sublane_bit, 1 << lane_bit
    one_tile = (1, SUBLANES, LANES)
    in_sublane = sublane_iota(one_tile) >> sublane_bit & 1
    in_lane = lane_iota(one_tile) >> lane_bit & 1
    flipped = jnp.where(in_sublane == 0, pltpu.roll(tiles, SUBLANES - step, 1), pltpu.roll(tiles, step, 1))
    if 2 * hop == LANES:
        flipped = pltpu.roll(flipped, hop, 2)
    else:
        flipped = jnp.where(in_lane == 0, pltpu.roll(flipped, LANES - hop, 2), pltpu.roll(flipped, hop, 2))
    return jnp.where(in_sublane == in_lane, tiles, flipped)


def shuffle(tiles):
    tiles = swap_sublane_lane(tiles, 0, 5)
    tiles = swap_sublane_lane(tiles, 1, 6)
    pairs = tiles.reshape(-1, 2, SUBLANES, LANES)
    even, odd = pairs[:, 0], pairs[:, 1]
    lower = sublane_iota((1, SUBLANES, LANES)) < SUBLANES // 2
    new_even = jnp.where(lower, even, pltpu.roll(odd, SUBLANES // 2, 1))
    new_odd = jnp.where(lower, pltpu.roll(even, SUBLANES // 2, 1), odd)
    return jnp.stack([new_even, new_odd], axis=1).reshape(tiles.shape)


def wide_gate(real, imag):
    return jnp.concatenate(
        [jnp.concatenate([real, -imag], axis=1), jnp.concatenate([imag, real], axis=1)], axis=0
    )


def take_lanes(array, index):
    rows = [
        jnp.take_along_axis(array[r : r + SUBLANES], index, axis=1) for r in range(0, array.shape[0], SUBLANES)
    ]
    return jnp.concatenate(rows, axis=0)


def apply_rows(tiles, gate):
    parts = tiles.reshape(2, TILES * SUBLANES, LANES)
    return product(jnp.concatenate([parts[0], parts[1]], axis=1), gate, ((1,), (1,)))


def apply_columns(tiles, gate):
    pairs = shuffle(tiles).reshape(TILES, 2, SUBLANES, LANES)
    columns = jnp.concatenate(
        [pairs[:, 0].reshape(WIDE, LANES), pairs[:, 1].reshape(WIDE, LANES)], axis=1
    )
    out = product(gate, columns, ((1,), (0,)))
    back = jnp.stack(
        [out[:, :LANES].reshape(TILES, SUBLANES, LANES), out[:, LANES:].reshape(TILES, SUBLANES, LANES)], axis=1
    )
    return shuffle(back.reshape(2 * TILES, SUBLANES, LANES))


def received_gate(gate_ref):
    real, imag = gate_ref[0], gate_ref[1]
    lane = lane_iota((SUBLANES, LANES))
    part = lane_iota((1, LANES)) >> 1 & 1
    blocks = []
    for half in range(2):
        index = half * (LANES // 2) + ((lane >> 2) << 1) + (lane & 1)
        real_half, imag_half = take_lanes(real, index), take_lanes(imag, index)
        blocks.append(
            jnp.concatenate(
                [jnp.where(part == 0, real_half, -imag_half), jnp.where(part == 0, imag_half, real_half)], axis=0
            )
        )
    return jnp.concatenate(blocks, axis=1)


def plan(perm_ref, cycle):
    one = jnp.int32(1)
    source = [perm_ref[cycle, b] for b in range(LANE_BITS + TILE_BITS)]
    crosses = [
        jnp.where(source[b] >= LANE_BITS, 1, 0) if b < LANE_BITS else jnp.where(source[b] < LANE_BITS, 1, 0)
        for b in range(LANE_BITS + TILE_BITS)
    ]
    count = sum(crosses[1:LANE_BITS], crosses[0])
    place = []
    for first, last in ((0, LANE_BITS), (LANE_BITS, LANE_BITS + TILE_BITS)):
        ahead = jnp.int32(0)
        for b in range(first, last):
            place.append(jnp.where(crosses[b] == 1, ahead, count + (b - first) - ahead))
            ahead = ahead + crosses[b]
    tile_from, tile_to = [], []
    for at in range(TILE_BITS):
        origin, target = jnp.int32(0), jnp.int32(0)
        for b in range(LANE_BITS + TILE_BITS):
            is_tile_source = source[b] >= LANE_BITS
            bit = lax.shift_left(one, jnp.maximum(source[b] - LANE_BITS, 0))
            origin = origin + jnp.where(jnp.logical_and(is_tile_source, place[b] == at), bit, 0)
            if b >= LANE_BITS:
                target = target + jnp.where(place[b] == at, 1 << (b - LANE_BITS), 0)
        tile_from.append(origin)
        tile_to.append(target)
    lane = lane_iota((SUBLANES, LANES))
    lane_from = jnp.zeros((SUBLANES, LANES), jnp.int32)
    lane_to = jnp.zeros((SUBLANES, LANES), jnp.int32)
    for b in range(LANE_BITS + TILE_BITS):
        bit = lax.shift_right_logical(lane, jnp.full((SUBLANES, LANES), place[b])) & 1
        shift = jnp.full((SUBLANES, LANES), jnp.where(source[b] < LANE_BITS, source[b], 0))
        keep = jnp.where(source[b] < LANE_BITS, 1, 0)
        lane_from = lane_from + lax.shift_left(bit * keep, shift)
        if b < LANE_BITS:
            lane_to = lane_to + (bit << b)
    return count, tile_from, tile_to, lane_from, lane_to


def combine(basis, value):
    total = jnp.int32(0)
    for bit in range(TILE_BITS):
        if value >> bit & 1:
            total = total + basis[bit]
    return total


def permute(load, store, scalars):
    count, tile_from, tile_to, lane_from, _ = scalars
    lane = lane_iota((SUBLANES, LANES))
    for part in range(2):
        tiles = [
            jnp.take_along_axis(load(part, combine(tile_from, at)), lane_from, axis=1) for at in range(TILES)
        ]
        for j in range(TILE_BITS):
            hop = 1 << j
            idle = jnp.full((SUBLANES, LANES), jnp.where(count > j, 0, 1)) == 1
            in_lane = lane >> j & 1
            keep_even = jnp.logical_or(in_lane == 0, idle)
            keep_odd = jnp.logical_or(in_lane == 1, idle)
            for at in range(TILES):
                if at & hop:
                    continue
                even, odd = tiles[at], tiles[at + hop]
                tiles[at] = jnp.where(keep_even, even, pltpu.roll(odd, hop, 1))
                tiles[at + hop] = jnp.where(keep_odd, odd, pltpu.roll(even, LANES - hop, 1))
        for at in range(TILES):
            store(part, combine(tile_to, at), tiles[at])


def local_gates(cycle, load, perm_ref, own_ref, gates, scratch, kept_ref, sent_ref):
    scalars = plan(perm_ref, cycle)

    def store(part, tile, value):
        scratch[part, tile] = value

    permute(load, store, scalars)
    lane_to = scalars[-1]
    first = wide_gate(take_lanes(gates[0, 0], lane_to), take_lanes(gates[0, 1], lane_to))
    out = apply_rows(scratch[...].reshape(2 * TILES, SUBLANES, LANES), first)
    tiles = jnp.concatenate(
        [out[:, :LANES].reshape(TILES, SUBLANES, LANES), out[:, LANES:].reshape(TILES, SUBLANES, LANES)], axis=0
    )
    tiles = apply_columns(tiles, wide_gate(gates[1, 0], gates[1, 1]))
    real, imag = gates[2, 0], gates[2, 1]
    cut = LANES // 2
    last = jnp.concatenate(
        [
            wide_gate(real, imag)[at : at + cut]
            for at in (0, LANES, cut, LANES + cut)
        ],
        axis=0,
    )
    out = apply_rows(tiles, last)
    kept_ref[:, 0] = out[:, :LANES].reshape(TILES, SUBLANES, LANES)
    kept_ref[:, 1] = out[:, LANES:].reshape(TILES, SUBLANES, LANES)
    sent_ref[...] = kept_ref[pl.ds((1 - own_ref[0]) * (TILES // 2), TILES // 2)]


def first_kernel(perm_ref, own_ref, state_ref, gates_ref, kept_ref, sent_ref, scratch):
    def load(part, tile):
        return state_ref[part, :, pl.ds(pl.multiple_of(tile * LANES, LANES), LANES)]

    local_gates(0, load, perm_ref, own_ref, gates_ref.at[0], scratch, kept_ref, sent_ref)


def middle_kernel(perm_ref, own_ref, tiles_ref, gates_ref, kept_ref, sent_ref, before, scratch):
    before[...] = apply_columns(tiles_ref[...], received_gate(gates_ref.at[0, 3])).reshape(before.shape)

    def load(part, tile):
        return before[part, tile]

    local_gates(1, load, perm_ref, own_ref, gates_ref.at[1], scratch, kept_ref, sent_ref)


def last_kernel(tiles_ref, gates_ref, out_ref):
    tiles = apply_columns(tiles_ref[...], received_gate(gates_ref.at[1, 3])).reshape(2, TILES, SUBLANES, LANES)
    for tile in range(TILES):
        out_ref[:, :, tile * LANES : (tile + 1) * LANES] = tiles[:, tile]


SMEM = pl.BlockSpec(memory_space=pltpu.SMEM)
VMEM = pl.BlockSpec(memory_space=pltpu.VMEM)
TILE_SHAPE = (2 * TILES, SUBLANES, LANES)
SCRATCH = pltpu.VMEM((2, TILES, SUBLANES, LANES), jnp.float32)
TO_SEND = (
    jax.ShapeDtypeStruct((TILES, 2, SUBLANES, LANES), jnp.float32),
    jax.ShapeDtypeStruct((TILES // 2, 2, SUBLANES, LANES), jnp.float32),
)


def exchange(kept, sent, own, which):
    pairs = [(i, i ^ 1 << which) for i in range(lax.axis_size("grp"))]
    received = lax.ppermute(sent, "grp", pairs)
    joined = lax.dynamic_update_slice(kept, received, ((1 - own) * (TILES // 2), 0, 0, 0))
    return lax.all_to_all(joined.reshape(TILE_SHAPE), "dev", split_axis=0, concat_axis=0, tiled=True)


def on_device(state, gates, local_perm):
    grp = lax.axis_index("grp")
    owns = [grp >> cycle & 1 for cycle in range(CYCLES)]
    kept, sent = pl.pallas_call(
        first_kernel,
        out_shape=TO_SEND,
        in_specs=[SMEM, SMEM, VMEM, VMEM],
        out_specs=(VMEM, VMEM),
        scratch_shapes=[SCRATCH],
    )(local_perm, owns[0].reshape(1), state, gates)
    tiles = exchange(kept, sent, owns[0], 0)
    kept, sent = pl.pallas_call(
        middle_kernel,
        out_shape=TO_SEND,
        in_specs=[SMEM, SMEM, VMEM, VMEM],
        out_specs=(VMEM, VMEM),
        scratch_shapes=[SCRATCH, SCRATCH],
    )(local_perm, owns[1].reshape(1), tiles, gates)
    tiles = exchange(kept, sent, owns[1], 1)
    return pl.pallas_call(
        last_kernel,
        out_shape=jax.ShapeDtypeStruct(state.shape, jnp.float32),
        in_specs=[VMEM, VMEM],
        out_specs=VMEM,
    )(tiles, gates)


def solution(mesh):
    placed = (P(None, None, ("grp", "dev")), P(), P())
    return jax.shard_map(
        on_device,
        mesh=mesh,
        in_specs=placed,
        out_specs=P(None, None, ("grp", "dev")),
        check_vma=False,
    )
```

```python
import functools

import jax
import jax.numpy as jnp
from jax import lax
from jax.experimental import pallas as pl
from jax.experimental.pallas import tpu as pltpu
from jax.sharding import Mesh, PartitionSpec as P

CYCLES = 2
LANE_BITS = 7
TILE_BITS = 5
TILES = 1 << TILE_BITS
SUBLANES = 8
LANES = 1 << LANE_BITS
WIDE = 2 * LANES


def lane_iota(shape):
    return lax.broadcasted_iota(jnp.int32, shape, len(shape) - 1)


def sublane_iota(shape):
    return lax.broadcasted_iota(jnp.int32, shape, len(shape) - 2)


def halves(array):
    high = array.astype(jnp.bfloat16)
    return high, (array - high.astype(jnp.float32)).astype(jnp.bfloat16)


def product(left, right, contract):
    left_high, left_low = halves(left)
    right_high, right_low = halves(right)
    dims = (contract, ((), ()))
    dot = functools.partial(lax.dot_general, dimension_numbers=dims, preferred_element_type=jnp.float32)
    return dot(left_high, right_high) + (dot(left_high, right_low) + dot(left_low, right_high))


def swap_sublane_lane(tiles, sublane_bit, lane_bit):
    step, hop = 1 << sublane_bit, 1 << lane_bit
    one_tile = (1, SUBLANES, LANES)
    in_sublane = sublane_iota(one_tile) >> sublane_bit & 1
    in_lane = lane_iota(one_tile) >> lane_bit & 1
    flipped = jnp.where(in_sublane == 0, pltpu.roll(tiles, SUBLANES - step, 1), pltpu.roll(tiles, step, 1))
    if 2 * hop == LANES:
        flipped = pltpu.roll(flipped, hop, 2)
    else:
        flipped = jnp.where(in_lane == 0, pltpu.roll(flipped, LANES - hop, 2), pltpu.roll(flipped, hop, 2))
    return jnp.where(in_sublane == in_lane, tiles, flipped)


def swap_sublane_tile(low, high, sublane_bit):
    step = 1 << sublane_bit
    clear = sublane_iota((1, SUBLANES, LANES)) >> sublane_bit & 1 == 0
    new_low = jnp.where(clear, low, pltpu.roll(high, step, 1))
    new_high = jnp.where(clear, pltpu.roll(low, SUBLANES - step, 1), high)
    return new_low, new_high


def shuffle(tiles):
    tiles = swap_sublane_lane(tiles, 0, 5)
    tiles = swap_sublane_lane(tiles, 1, 6)
    pairs = tiles.reshape(-1, 2, SUBLANES, LANES)
    return jnp.stack(swap_sublane_tile(pairs[:, 0], pairs[:, 1], 2), axis=1).reshape(tiles.shape)


def wide_gate(real, imag):
    return jnp.concatenate(
        [jnp.concatenate([real, -imag], axis=1), jnp.concatenate([imag, real], axis=1)], axis=0
    )


def take_lanes(array, index):
    rows = [
        jnp.take_along_axis(array[r : r + SUBLANES], index, axis=1) for r in range(0, array.shape[0], SUBLANES)
    ]
    return jnp.concatenate(rows, axis=0)


def apply_rows(tiles, gate):
    parts = tiles.reshape(2, TILES * SUBLANES, LANES)
    return product(jnp.concatenate([parts[0], parts[1]], axis=1), gate, ((1,), (1,)))


def apply_columns(tiles, gate):
    pairs = shuffle(tiles).reshape(TILES, 2, SUBLANES, LANES)
    columns = jnp.concatenate(
        [pairs[:, 0].reshape(WIDE, LANES), pairs[:, 1].reshape(WIDE, LANES)], axis=1
    )
    out = product(gate, columns, ((1,), (0,)))
    back = jnp.stack(
        [out[:, :LANES].reshape(TILES, SUBLANES, LANES), out[:, LANES:].reshape(TILES, SUBLANES, LANES)], axis=1
    )
    return shuffle(back.reshape(2 * TILES, SUBLANES, LANES))


def interleaved_gate(real, imag, index_of, part_bit):
    lane = lane_iota((SUBLANES, LANES))
    part = lane_iota((1, LANES)) >> part_bit & 1
    blocks = []
    for half in range(2):
        index = index_of(half, lane)
        real_half, imag_half = take_lanes(real, index), take_lanes(imag, index)
        blocks.append(
            jnp.concatenate(
                [jnp.where(part == 0, real_half, -imag_half), jnp.where(part == 0, imag_half, real_half)], axis=0
            )
        )
    return jnp.concatenate(blocks, axis=1)


def middle_gate(gate_ref):
    def index_of(half, lane):
        return half * (LANES // 2) + ((lane >> 2) << 1) + (lane & 1)

    return interleaved_gate(gate_ref[0], gate_ref[1], index_of, 1)


def swap_middle_rows(array):
    tiles = array.reshape(-1, SUBLANES, LANES)
    row = sublane_iota((1, SUBLANES, LANES)) >> 1 & 3
    tiles = jnp.where(
        row == 1, pltpu.roll(tiles, SUBLANES - 2, 1), jnp.where(row == 2, pltpu.roll(tiles, 2, 1), tiles)
    )
    return tiles.reshape(array.shape)


def last_gate(gate_ref):
    def index_of(half, lane):
        return ((lane >> 1 & 1) << 6) + half * (LANES // 4) + ((lane >> 3) << 1) + (lane & 1)

    return interleaved_gate(swap_middle_rows(gate_ref[0]), swap_middle_rows(gate_ref[1]), index_of, 2)


def plan(perm_ref, cycle):
    one = jnp.int32(1)
    source = [perm_ref[cycle, b] for b in range(LANE_BITS + TILE_BITS)]
    crosses = [
        jnp.where(source[b] >= LANE_BITS, 1, 0) if b < LANE_BITS else jnp.where(source[b] < LANE_BITS, 1, 0)
        for b in range(LANE_BITS + TILE_BITS)
    ]
    count = sum(crosses[1:LANE_BITS], crosses[0])
    place = []
    for first, last in ((0, LANE_BITS), (LANE_BITS, LANE_BITS + TILE_BITS)):
        ahead = jnp.int32(0)
        for b in range(first, last):
            place.append(jnp.where(crosses[b] == 1, ahead, count + (b - first) - ahead))
            ahead = ahead + crosses[b]
    tile_from, tile_to = [], []
    for at in range(TILE_BITS):
        origin, target = jnp.int32(0), jnp.int32(0)
        for b in range(LANE_BITS + TILE_BITS):
            is_tile_source = source[b] >= LANE_BITS
            bit = lax.shift_left(one, jnp.maximum(source[b] - LANE_BITS, 0))
            origin = origin + jnp.where(jnp.logical_and(is_tile_source, place[b] == at), bit, 0)
            if b >= LANE_BITS:
                target = target + jnp.where(place[b] == at, 1 << (b - LANE_BITS), 0)
        tile_from.append(origin)
        tile_to.append(target)
    lane = lane_iota((SUBLANES, LANES))
    lane_from = jnp.zeros((SUBLANES, LANES), jnp.int32)
    lane_to = jnp.zeros((SUBLANES, LANES), jnp.int32)
    for b in range(LANE_BITS + TILE_BITS):
        bit = lax.shift_right_logical(lane, jnp.full((SUBLANES, LANES), place[b])) & 1
        shift = jnp.full((SUBLANES, LANES), jnp.where(source[b] < LANE_BITS, source[b], 0))
        keep = jnp.where(source[b] < LANE_BITS, 1, 0)
        lane_from = lane_from + lax.shift_left(bit * keep, shift)
        if b < LANE_BITS:
            lane_to = lane_to + (bit << b)
    return count, tile_from, tile_to, lane_from, lane_to


def combine(basis, value):
    total = jnp.int32(0)
    for bit in range(TILE_BITS):
        if value >> bit & 1:
            total = total + basis[bit]
    return total


def permute(load, store, scalars):
    count, tile_from, tile_to, lane_from, _ = scalars
    lane = lane_iota((SUBLANES, LANES))
    for part in range(2):
        tiles = [
            jnp.take_along_axis(load(part, combine(tile_from, at)), lane_from, axis=1) for at in range(TILES)
        ]
        for j in range(TILE_BITS):
            hop = 1 << j
            idle = jnp.full((SUBLANES, LANES), jnp.where(count > j, 0, 1)) == 1
            in_lane = lane >> j & 1
            keep_even = jnp.logical_or(in_lane == 0, idle)
            keep_odd = jnp.logical_or(in_lane == 1, idle)
            for at in range(TILES):
                if at & hop:
                    continue
                even, odd = tiles[at], tiles[at + hop]
                tiles[at] = jnp.where(keep_even, even, pltpu.roll(odd, hop, 1))
                tiles[at + hop] = jnp.where(keep_odd, odd, pltpu.roll(even, LANES - hop, 1))
        for at in range(TILES):
            store(part, combine(tile_to, at), tiles[at])


def local_gates(cycle, load, perm_ref, gates, scratch, out_ref, sublane_bit):
    scalars = plan(perm_ref, cycle)

    def store(part, tile, value):
        scratch[part, tile] = value

    permute(load, store, scalars)
    lane_to = scalars[-1]
    first = wide_gate(take_lanes(gates[0, 0], lane_to), take_lanes(gates[0, 1], lane_to))
    out = apply_rows(scratch[...].reshape(2 * TILES, SUBLANES, LANES), first)
    tiles = jnp.concatenate(
        [out[:, :LANES].reshape(TILES, SUBLANES, LANES), out[:, LANES:].reshape(TILES, SUBLANES, LANES)], axis=0
    )
    tiles = apply_columns(tiles, wide_gate(gates[1, 0], gates[1, 1]))
    gate = wide_gate(gates[2, 0], gates[2, 1])
    cut = LANES // 2
    gate = jnp.concatenate([gate[at : at + cut] for at in (0, LANES, cut, LANES + cut)], axis=0)
    out = apply_rows(tiles, gate)
    for bit in range(2):
        piece = out[:, bit * LANES : (bit + 1) * LANES].reshape(2, TILES // 2, SUBLANES, LANES)
        out_ref[0, :, bit], out_ref[1, :, bit] = swap_sublane_tile(piece[0], piece[1], sublane_bit)


def first_kernel(perm_ref, state_ref, gates_ref, out_ref, scratch):
    def load(part, tile):
        return state_ref[part, :, pl.ds(pl.multiple_of(tile * LANES, LANES), LANES)]

    local_gates(0, load, perm_ref, gates_ref.at[0], scratch, out_ref, 1)


def middle_kernel(perm_ref, tiles_ref, gates_ref, out_ref, before, scratch):
    before[...] = apply_columns(tiles_ref[...], middle_gate(gates_ref.at[0, 3])).reshape(before.shape)

    def load(part, tile):
        return before[part, tile]

    local_gates(1, load, perm_ref, gates_ref.at[1], scratch, out_ref, 2)


def last_kernel(tiles_ref, gates_ref, out_ref):
    tiles = swap_sublane_lane(swap_sublane_lane(tiles_ref[...], 0, 5), 2, 6)
    columns = jnp.concatenate([tiles[:TILES].reshape(WIDE, LANES), tiles[TILES:].reshape(WIDE, LANES)], axis=1)
    out = product(last_gate(gates_ref.at[1, 3]), columns, ((1,), (0,)))
    sides = [
        swap_sublane_lane(out[:, at : at + LANES].reshape(TILES, SUBLANES, LANES), 0, 5) for at in (0, LANES)
    ]
    for bit, side in enumerate(swap_sublane_tile(sides[0], sides[1], 1)):
        side = swap_sublane_lane(side, 2, 6)
        for at in range(TILES):
            part, tile = at // (TILES // 2), 2 * (at % (TILES // 2)) + bit
            out_ref[part, :, tile * LANES : (tile + 1) * LANES] = side[at]


SMEM = pl.BlockSpec(memory_space=pltpu.SMEM)
VMEM = pl.BlockSpec(memory_space=pltpu.VMEM)
TILE_SHAPE = (2 * TILES, SUBLANES, LANES)
SCRATCH = pltpu.VMEM((2, TILES, SUBLANES, LANES), jnp.float32)
TO_SEND = jax.ShapeDtypeStruct((2, TILES // 2, 2, SUBLANES, LANES), jnp.float32)


def exchange(tiles, axes):
    ways = 1
    for axis in axes:
        ways *= lax.axis_size(axis)
    chunks = tiles.reshape(ways, -1, LANES)
    return lax.all_to_all(chunks, axes, split_axis=0, concat_axis=0, tiled=True).reshape(TILE_SHAPE)


def on_device(state, gates, local_perm):
    tiles = pl.pallas_call(
        first_kernel,
        out_shape=TO_SEND,
        in_specs=[SMEM, VMEM, VMEM],
        out_specs=VMEM,
        scratch_shapes=[SCRATCH],
    )(local_perm, state, gates)
    tiles = exchange(tiles, ("dev", "grp1", "grp0"))
    tiles = pl.pallas_call(
        middle_kernel,
        out_shape=TO_SEND,
        in_specs=[SMEM, VMEM, VMEM],
        out_specs=VMEM,
        scratch_shapes=[SCRATCH, SCRATCH],
    )(local_perm, tiles, gates)
    tiles = exchange(tiles, ("dev", "grp1"))
    return pl.pallas_call(
        last_kernel,
        out_shape=jax.ShapeDtypeStruct(state.shape, jnp.float32),
        in_specs=[VMEM, VMEM],
        out_specs=VMEM,
    )(tiles, gates)


def solution(mesh):
    groups, devs = mesh.devices.shape
    split = Mesh(mesh.devices.reshape(groups // 4, 2, 2, devs), ("grp_rest", "grp1", "grp0", "dev"))
    placed = P(None, None, ("grp_rest", "grp1", "grp0", "dev"))
    return jax.shard_map(
        on_device,
        mesh=split,
        in_specs=(placed, P(), P()),
        out_specs=placed,
        check_vma=False,
    )
```

```python
import functools

import jax
import jax.numpy as jnp
from jax import lax
from jax.experimental import pallas as pl
from jax.experimental.pallas import tpu as pltpu
from jax.sharding import Mesh, PartitionSpec as P

CYCLES = 2
LANE_BITS = 7
TILE_BITS = 5
TILES = 1 << TILE_BITS
SUBLANES = 8
LANES = 1 << LANE_BITS
WIDE = 2 * LANES


def lane_iota(shape):
    return lax.broadcasted_iota(jnp.int32, shape, len(shape) - 1)


def sublane_iota(shape):
    return lax.broadcasted_iota(jnp.int32, shape, len(shape) - 2)


def halves(array):
    high = array.astype(jnp.bfloat16)
    return high, (array - high.astype(jnp.float32)).astype(jnp.bfloat16)


def product(left, right, contract):
    left_high, left_low = left
    right_high, right_low = right
    dims = (contract, ((), ()))
    dot = functools.partial(lax.dot_general, dimension_numbers=dims, preferred_element_type=jnp.float32)
    return dot(left_high, right_high) + (dot(left_high, right_low) + dot(left_low, right_high))


def flip_lane_bit(tiles, lane_bit):
    hop = 1 << lane_bit
    if 2 * hop == LANES:
        return pltpu.roll(tiles, hop, 2)
    index = lane_iota((SUBLANES, LANES)) ^ hop
    return jnp.stack([jnp.take_along_axis(tiles[at], index, axis=1) for at in range(tiles.shape[0])])


def swap_sublane_lane(tiles, sublane_bit, lane_bit):
    step = 1 << sublane_bit
    one_tile = (1, SUBLANES, LANES)
    in_sublane = sublane_iota(one_tile) >> sublane_bit & 1
    in_lane = lane_iota(one_tile) >> lane_bit & 1
    if 2 * step == SUBLANES:
        flipped = pltpu.roll(tiles, step, 1)
    else:
        flipped = jnp.where(in_sublane == 0, pltpu.roll(tiles, SUBLANES - step, 1), pltpu.roll(tiles, step, 1))
    return jnp.where(in_sublane == in_lane, tiles, flip_lane_bit(flipped, lane_bit))


def swap_sublane_tile(low, high, sublane_bit):
    step = 1 << sublane_bit
    clear = sublane_iota((1, SUBLANES, LANES)) >> sublane_bit & 1 == 0
    new_low = jnp.where(clear, low, pltpu.roll(high, step, 1))
    new_high = jnp.where(clear, pltpu.roll(low, SUBLANES - step, 1), high)
    return new_low, new_high


def shuffle(tiles):
    tiles = swap_sublane_lane(tiles, 0, 5)
    tiles = swap_sublane_lane(tiles, 1, 6)
    pairs = tiles.reshape(-1, 2, SUBLANES, LANES)
    return jnp.stack(swap_sublane_tile(pairs[:, 0], pairs[:, 1], 2), axis=1).reshape(tiles.shape)


def wide_gate(real, imag):
    return jnp.concatenate(
        [jnp.concatenate([real, -imag], axis=1), jnp.concatenate([imag, real], axis=1)], axis=0
    )


def sending_gate(real, imag):
    gate = wide_gate(real, imag)
    cut = LANES // 2
    return jnp.concatenate([gate[at : at + cut] for at in (0, LANES, cut, LANES + cut)], axis=0)


def take_lanes(array, index):
    rows = [
        jnp.take_along_axis(array[r : r + SUBLANES], index, axis=1) for r in range(0, array.shape[0], SUBLANES)
    ]
    return jnp.concatenate(rows, axis=0)


def apply_rows(tiles, gate):
    parts = tiles.reshape(2, TILES * SUBLANES, LANES)
    return product(halves(jnp.concatenate([parts[0], parts[1]], axis=1)), gate, ((1,), (1,)))


def apply_columns(tiles, gate):
    pairs = shuffle(tiles).reshape(TILES, 2, SUBLANES, LANES)
    columns = jnp.concatenate(
        [pairs[:, 0].reshape(WIDE, LANES), pairs[:, 1].reshape(WIDE, LANES)], axis=1
    )
    out = product(gate, halves(columns), ((1,), (0,)))
    back = jnp.stack(
        [out[:, :LANES].reshape(TILES, SUBLANES, LANES), out[:, LANES:].reshape(TILES, SUBLANES, LANES)], axis=1
    )
    return shuffle(back.reshape(2 * TILES, SUBLANES, LANES))


def interleaved_gate(real, imag, index_of, part_bit):
    lane = lane_iota((SUBLANES, LANES))
    part = lane_iota((1, LANES)) >> part_bit & 1
    blocks = []
    for half in range(2):
        index = index_of(half, lane)
        real_half, imag_half = take_lanes(real, index), take_lanes(imag, index)
        blocks.append(
            jnp.concatenate(
                [jnp.where(part == 0, real_half, -imag_half), jnp.where(part == 0, imag_half, real_half)], axis=0
            )
        )
    return jnp.concatenate(blocks, axis=1)


def middle_gate(gate_ref):
    def index_of(half, lane):
        return half * (LANES // 2) + ((lane >> 2) << 1) + (lane & 1)

    return interleaved_gate(gate_ref[0], gate_ref[1], index_of, 1)


def swap_middle_rows(array):
    tiles = array.reshape(-1, SUBLANES, LANES)
    row = sublane_iota((1, SUBLANES, LANES)) >> 1 & 3
    tiles = jnp.where(
        row == 1, pltpu.roll(tiles, SUBLANES - 2, 1), jnp.where(row == 2, pltpu.roll(tiles, 2, 1), tiles)
    )
    return tiles.reshape(array.shape)


def last_gate(gate_ref):
    def index_of(half, lane):
        return ((lane >> 1 & 1) << 6) + half * (LANES // 4) + ((lane >> 3) << 1) + (lane & 1)

    return interleaved_gate(swap_middle_rows(gate_ref[0]), swap_middle_rows(gate_ref[1]), index_of, 2)


def wire_place(tile):
    z, low = tile >> 2, tile & 3
    return (z & 1) << 5 | (z >> 1 & 1) << 4 | (z >> 2 & 1) << 3 | (z >> 3 & 1) << 2 | low


def arrived_tiles(tiles_ref):
    return jnp.stack([tiles_ref[wire_place(tile)] for tile in range(2 * TILES)])


OUT_OF = 0
CROSSING = OUT_OF + LANE_BITS + TILE_BITS
LANE_OF = CROSSING + TILE_BITS + 1
TABLE = pltpu.SMEM((LANE_OF + LANE_BITS + TILE_BITS,), jnp.int32)


def plan(perm_ref, cycle, table):
    source = [perm_ref[cycle, b] for b in range(LANE_BITS + TILE_BITS)]
    for b in range(LANE_BITS + TILE_BITS):
        table[OUT_OF + source[b]] = jnp.int32(b)
    count = jnp.int32(0)
    for b in range(LANE_BITS, LANE_BITS + TILE_BITS):
        table[CROSSING + count] = jnp.int32(b)
        count = count + jnp.where(source[b] < LANE_BITS, 1, 0)
    for b in range(LANE_BITS):
        table[LANE_OF + b] = jnp.int32(b)
    rank = jnp.int32(0)
    bits = []
    for q in range(TILE_BITS):
        out = table[OUT_OF + LANE_BITS + q]
        crosses = out < LANE_BITS
        partner = table[CROSSING + jnp.where(crosses, rank, 0)]
        rank = rank + jnp.where(crosses, 1, 0)
        origin = perm_ref[cycle, partner]
        table[LANE_OF + LANE_BITS + q] = origin
        target = jnp.where(crosses, partner, out) - LANE_BITS
        bits.append((crosses, out, origin, target))
    lanes = [table[LANE_OF + source[b]] for b in range(LANE_BITS)]
    return bits, lanes


def combine(basis, value):
    total = jnp.int32(0)
    for bit in range(TILE_BITS):
        if value >> bit & 1:
            total = total + basis[bit]
    return total


def permute(load, store, plans):
    bits, lanes = plans
    lane = lane_iota((SUBLANES, LANES))

    def shifted(amount):
        return lax.shift_right_logical(lane, jnp.full((SUBLANES, LANES), amount)) & 1

    never = 31
    before = [shifted(jnp.where(crosses, origin, never)) == 1 for crosses, _, origin, _ in bits]
    after = [shifted(jnp.where(crosses, out, never)) == 1 for crosses, out, _, _ in bits]
    index = jnp.zeros((SUBLANES, LANES), jnp.int32)
    for b in range(LANE_BITS):
        index = index + lax.shift_left(lane >> b & 1, jnp.full((SUBLANES, LANES), lanes[b]))
    flips = [jnp.where(crosses, lax.shift_left(jnp.int32(1), origin), 0) for crosses, _, origin, _ in bits]
    targets = [lax.shift_left(jnp.int32(1), target) for _, _, _, target in bits]

    def trade(tiles, masks):
        for q in range(TILE_BITS):
            for at in range(TILES):
                if not at >> q & 1:
                    low, high = tiles[at], tiles[at + (1 << q)]
                    tiles[at] = jnp.where(masks[q], high, low)
                    tiles[at + (1 << q)] = jnp.where(masks[q], low, high)
        return tiles

    for part in range(2):
        tiles = trade([load(part, at) for at in range(TILES)], before)
        tiles = [
            jnp.take_along_axis(tiles[at], index ^ jnp.full((SUBLANES, LANES), combine(flips, at)), axis=1)
            for at in range(TILES)
        ]
        for at, tile in enumerate(trade(tiles, after)):
            store(part, combine(targets, at), tile)


def local_gates(plans, load, gates, scratch, out_ref, sublane_bit):
    def store(part, tile, value):
        scratch[part, tile] = value

    permute(load, store, plans)
    out = apply_rows(scratch[...].reshape(2 * TILES, SUBLANES, LANES), gates(0))
    tiles = jnp.concatenate(
        [out[:, :LANES].reshape(TILES, SUBLANES, LANES), out[:, LANES:].reshape(TILES, SUBLANES, LANES)], axis=0
    )
    tiles = apply_columns(tiles, gates(1))
    out = apply_rows(tiles, gates(2))
    for bit in range(2):
        piece = out[:, bit * LANES : (bit + 1) * LANES].reshape(2, TILES // 2, SUBLANES, LANES)
        for top, swapped in enumerate(swap_sublane_tile(piece[0], piece[1], sublane_bit)):
            for at in range(TILES // 2):
                out_ref[wire_place(top * TILES + 2 * at + bit)] = swapped[at]


def first_kernel(perm_ref, state_hbm, gates_hbm, out_ref, state_ref, gates_ref, scratch, table, arrived):
    copies = [pltpu.make_async_copy(state_hbm, state_ref, arrived.at[0])]
    for which in range(3):
        copies.append(pltpu.make_async_copy(gates_hbm.at[0, which], gates_ref.at[which], arrived.at[1 + which]))
    for copy in copies:
        copy.start()
    plans = plan(perm_ref, 0, table)
    copies[0].wait()

    def load(part, tile):
        return state_ref[part, :, tile * LANES : (tile + 1) * LANES]

    def gates(which):
        copies[1 + which].wait()
        form = sending_gate if which == 2 else wide_gate
        return halves(form(gates_ref[which, 0], gates_ref[which, 1]))

    local_gates(plans, load, gates, scratch, out_ref, 1)


def gate_kernel(gates_ref, out_ref):
    ready = [
        middle_gate(gates_ref.at[0, 3]),
        wide_gate(gates_ref[1, 0, 0], gates_ref[1, 0, 1]),
        wide_gate(gates_ref[1, 1, 0], gates_ref[1, 1, 1]),
        sending_gate(gates_ref[1, 2, 0], gates_ref[1, 2, 1]),
        last_gate(gates_ref.at[1, 3]),
    ]
    for at, gate in enumerate(ready):
        out_ref[at, 0], out_ref[at, 1] = halves(gate)


def middle_kernel(perm_ref, tiles_ref, gates_ref, out_ref, before, scratch, table):
    plans = plan(perm_ref, 1, table)

    def gates(which):
        return gates_ref[1 + which, 0], gates_ref[1 + which, 1]

    before[...] = apply_columns(arrived_tiles(tiles_ref), gates(-1)).reshape(before.shape)

    def load(part, tile):
        return before[part, tile]

    local_gates(plans, load, gates, scratch, out_ref, 2)


def last_kernel(tiles_ref, gates_ref, out_ref):
    tiles = swap_sublane_lane(swap_sublane_lane(arrived_tiles(tiles_ref), 0, 5), 2, 6)
    columns = jnp.concatenate([tiles[:TILES].reshape(WIDE, LANES), tiles[TILES:].reshape(WIDE, LANES)], axis=1)
    out = product((gates_ref[4, 0], gates_ref[4, 1]), halves(columns), ((1,), (0,)))
    sides = [
        swap_sublane_lane(out[:, at : at + LANES].reshape(TILES, SUBLANES, LANES), 0, 5) for at in (0, LANES)
    ]
    for bit, side in enumerate(swap_sublane_tile(sides[0], sides[1], 1)):
        side = swap_sublane_lane(side, 2, 6)
        for at in range(TILES):
            part, tile = at // (TILES // 2), 2 * (at % (TILES // 2)) + bit
            out_ref[part, :, tile * LANES : (tile + 1) * LANES] = side[at]


SMEM = pl.BlockSpec(memory_space=pltpu.SMEM)
HBM = pl.BlockSpec(memory_space=pltpu.HBM)
VMEM = pl.BlockSpec(memory_space=pltpu.VMEM)
ALL_VMEM = pltpu.CompilerParams(vmem_limit_bytes=67043328)
PARAMS = pltpu.CompilerParams(vmem_limit_bytes=12 << 20)
TILE_SHAPE = (2 * TILES, SUBLANES, LANES)
SCRATCH = pltpu.VMEM((2, TILES, SUBLANES, LANES), jnp.float32)
READY = jax.ShapeDtypeStruct((5, 2, WIDE, WIDE), jnp.bfloat16)
TO_SEND = jax.ShapeDtypeStruct(TILE_SHAPE, jnp.float32)
DEV = ("z0", "z1", "z2", "z3", "dev_low")


def exchange(tiles, axes):
    ways = 1
    for axis in axes:
        ways *= lax.axis_size(axis)
    chunks = tiles.reshape(ways, -1, LANES)
    return lax.all_to_all(chunks, axes, split_axis=0, concat_axis=0, tiled=True).reshape(TILE_SHAPE)


def on_device(state, gates, local_perm):
    tiles = pl.pallas_call(
        first_kernel,
        out_shape=TO_SEND,
        in_specs=[SMEM, HBM, HBM],
        out_specs=VMEM,
        scratch_shapes=[
            pltpu.VMEM(state.shape, jnp.float32),
            pltpu.VMEM((3,) + gates.shape[2:], jnp.float32),
            SCRATCH,
            TABLE,
            pltpu.SemaphoreType.DMA((4,)),
        ],
        compiler_params=ALL_VMEM,
    )(local_perm, state, gates)
    ready = pl.pallas_call(
        gate_kernel,
        out_shape=READY,
        in_specs=[VMEM],
        out_specs=VMEM,
        compiler_params=PARAMS,
        cost_estimate=pl.CostEstimate(flops=10**8, bytes_accessed=4 * 10**6, transcendentals=0),
    )(gates)
    tiles = exchange(tiles, DEV + ("grp1", "grp0"))
    tiles = pl.pallas_call(
        middle_kernel,
        out_shape=TO_SEND,
        in_specs=[SMEM, VMEM, VMEM],
        out_specs=VMEM,
        scratch_shapes=[SCRATCH, SCRATCH, TABLE],
        compiler_params=PARAMS,
    )(local_perm, tiles, ready)
    tiles = exchange(tiles, DEV + ("grp1",))
    return pl.pallas_call(
        last_kernel,
        out_shape=jax.ShapeDtypeStruct(state.shape, jnp.float32),
        in_specs=[VMEM, VMEM],
        out_specs=VMEM,
        compiler_params=PARAMS,
    )(tiles, ready)


def solution(mesh):
    groups, devs = mesh.devices.shape
    names = ("grp_rest", "grp1", "grp0", "z3", "z2", "z1", "z0", "dev_low")
    split = Mesh(mesh.devices.reshape(groups // 4, 2, 2, 2, 2, 2, 2, devs // 16), names)
    placed = P(None, None, names)
    return jax.shard_map(
        on_device,
        mesh=split,
        in_specs=(placed, P(), P()),
        out_specs=placed,
        check_vma=False,
    )
```

```python
import functools

import jax
import jax.numpy as jnp
from jax import lax
from jax.experimental import pallas as pl
from jax.experimental.pallas import tpu as pltpu
from jax.sharding import Mesh, PartitionSpec as P

CYCLES = 2
LANE_BITS = 7
TILE_BITS = 5
TILES = 1 << TILE_BITS
SUBLANES = 8
LANES = 1 << LANE_BITS
WIDE = 2 * LANES
ROW_SPLIT = 2


def lane_iota(shape):
    return lax.broadcasted_iota(jnp.int32, shape, len(shape) - 1)


def sublane_iota(shape):
    return lax.broadcasted_iota(jnp.int32, shape, len(shape) - 2)


def halves(array):
    high = array.astype(jnp.bfloat16)
    return high, (array - high.astype(jnp.float32)).astype(jnp.bfloat16)


def product(left, right, contract):
    left_high, left_low = left
    right_high, right_low = right
    dims = (contract, ((), ()))
    dot = functools.partial(lax.dot_general, dimension_numbers=dims, preferred_element_type=jnp.float32)
    return dot(left_high, right_high) + (dot(left_high, right_low) + dot(left_low, right_high))


def flip_lane_bit(tiles, lane_bit):
    hop = 1 << lane_bit
    if 2 * hop == LANES:
        return pltpu.roll(tiles, hop, 2)
    index = lane_iota((SUBLANES, LANES)) ^ hop
    return jnp.stack([jnp.take_along_axis(tiles[at], index, axis=1) for at in range(tiles.shape[0])])


def swap_sublane_lane(tiles, sublane_bit, lane_bit):
    step = 1 << sublane_bit
    one_tile = (1, SUBLANES, LANES)
    in_sublane = sublane_iota(one_tile) >> sublane_bit & 1
    in_lane = lane_iota(one_tile) >> lane_bit & 1
    if 2 * step == SUBLANES:
        flipped = pltpu.roll(tiles, step, 1)
    else:
        flipped = jnp.where(in_sublane == 0, pltpu.roll(tiles, SUBLANES - step, 1), pltpu.roll(tiles, step, 1))
    return jnp.where(in_sublane == in_lane, tiles, flip_lane_bit(flipped, lane_bit))


def swap_sublane_tile(low, high, sublane_bit):
    step = 1 << sublane_bit
    clear = sublane_iota((1, SUBLANES, LANES)) >> sublane_bit & 1 == 0
    new_low = jnp.where(clear, low, pltpu.roll(high, step, 1))
    new_high = jnp.where(clear, pltpu.roll(low, SUBLANES - step, 1), high)
    return new_low, new_high


def shuffle(tiles):
    tiles = swap_sublane_lane(tiles, 0, 5)
    tiles = swap_sublane_lane(tiles, 1, 6)
    pairs = tiles.reshape(-1, 2, SUBLANES, LANES)
    return jnp.stack(swap_sublane_tile(pairs[:, 0], pairs[:, 1], 2), axis=1).reshape(tiles.shape)


def wide_gate(real, imag):
    return jnp.concatenate(
        [jnp.concatenate([real, -imag], axis=1), jnp.concatenate([imag, real], axis=1)], axis=0
    )


def sending_gate(real, imag):
    gate = wide_gate(real, imag)
    cut = LANES // 2
    return jnp.concatenate([gate[at : at + cut] for at in (0, LANES, cut, LANES + cut)], axis=0)


def take_lanes(array, index):
    rows = [
        jnp.take_along_axis(array[r : r + SUBLANES], index, axis=1) for r in range(0, array.shape[0], SUBLANES)
    ]
    return jnp.concatenate(rows, axis=0)


def apply_rows(tiles, gate):
    parts = tiles.reshape(2, TILES * SUBLANES, LANES)
    rows = TILES * SUBLANES // ROW_SPLIT
    return jnp.concatenate(
        [
            product(
                halves(jnp.concatenate([parts[0, at : at + rows], parts[1, at : at + rows]], axis=1)), gate, ((1,), (1,))
            )
            for at in range(0, TILES * SUBLANES, rows)
        ],
        axis=0,
    )


def apply_columns(tiles, gate):
    pairs = shuffle(tiles).reshape(TILES, 2, SUBLANES, LANES)
    columns = jnp.concatenate(
        [pairs[:, 0].reshape(WIDE, LANES), pairs[:, 1].reshape(WIDE, LANES)], axis=1
    )
    out = product(gate, halves(columns), ((1,), (0,)))
    back = jnp.stack(
        [out[:, :LANES].reshape(TILES, SUBLANES, LANES), out[:, LANES:].reshape(TILES, SUBLANES, LANES)], axis=1
    )
    return shuffle(back.reshape(2 * TILES, SUBLANES, LANES))


def interleaved_gate(real, imag, index_of, part_bit):
    lane = lane_iota((SUBLANES, LANES))
    part = lane_iota((1, LANES)) >> part_bit & 1
    blocks = []
    for half in range(2):
        index = index_of(half, lane)
        real_half, imag_half = take_lanes(real, index), take_lanes(imag, index)
        blocks.append(
            jnp.concatenate(
                [jnp.where(part == 0, real_half, -imag_half), jnp.where(part == 0, imag_half, real_half)], axis=0
            )
        )
    return jnp.concatenate(blocks, axis=1)


def middle_gate(gate_ref):
    def index_of(half, lane):
        return half * (LANES // 2) + ((lane >> 2) << 1) + (lane & 1)

    return interleaved_gate(gate_ref[0], gate_ref[1], index_of, 1)


def swap_middle_rows(array):
    tiles = array.reshape(-1, SUBLANES, LANES)
    row = sublane_iota((1, SUBLANES, LANES)) >> 1 & 3
    tiles = jnp.where(
        row == 1, pltpu.roll(tiles, SUBLANES - 2, 1), jnp.where(row == 2, pltpu.roll(tiles, 2, 1), tiles)
    )
    return tiles.reshape(array.shape)


def last_gate(gate_ref):
    def index_of(half, lane):
        return ((lane >> 1 & 1) << 6) + half * (LANES // 4) + ((lane >> 3) << 1) + (lane & 1)

    return interleaved_gate(swap_middle_rows(gate_ref[0]), swap_middle_rows(gate_ref[1]), index_of, 2)


def wire_place(tile):
    z, low = tile >> 2, tile & 3
    return (z & 1) << 5 | (z >> 1 & 1) << 4 | (z >> 2 & 1) << 3 | (z >> 3 & 1) << 2 | low


def arrived_tiles(tiles_ref):
    return jnp.stack([tiles_ref[wire_place(tile)] for tile in range(2 * TILES)])


OUT_OF = 0
CROSSING = OUT_OF + LANE_BITS + TILE_BITS
LANE_OF = CROSSING + TILE_BITS + 1
TABLE = pltpu.SMEM((LANE_OF + LANE_BITS + TILE_BITS,), jnp.int32)


def plan(perm_ref, cycle, table):
    source = [perm_ref[cycle, b] for b in range(LANE_BITS + TILE_BITS)]
    for b in range(LANE_BITS + TILE_BITS):
        table[OUT_OF + source[b]] = jnp.int32(b)
    count = jnp.int32(0)
    for b in range(LANE_BITS, LANE_BITS + TILE_BITS):
        table[CROSSING + count] = jnp.int32(b)
        count = count + jnp.where(source[b] < LANE_BITS, 1, 0)
    for b in range(LANE_BITS):
        table[LANE_OF + b] = jnp.int32(b)
    rank = jnp.int32(0)
    bits = []
    for q in range(TILE_BITS):
        out = table[OUT_OF + LANE_BITS + q]
        crosses = out < LANE_BITS
        partner = table[CROSSING + jnp.where(crosses, rank, 0)]
        rank = rank + jnp.where(crosses, 1, 0)
        origin = perm_ref[cycle, partner]
        table[LANE_OF + LANE_BITS + q] = origin
        target = jnp.where(crosses, partner, out) - LANE_BITS
        bits.append((crosses, out, origin, target))
    lanes = [table[LANE_OF + source[b]] for b in range(LANE_BITS)]
    return bits, lanes


def combine(basis, value):
    total = jnp.int32(0)
    for bit in range(TILE_BITS):
        if value >> bit & 1:
            total = total + basis[bit]
    return total


def permute(load, store, plans):
    bits, lanes = plans
    lane = lane_iota((SUBLANES, LANES))

    def shifted(amount):
        return lax.shift_right_logical(lane, jnp.full((SUBLANES, LANES), amount)) & 1

    never = 31
    before = [shifted(jnp.where(crosses, origin, never)) == 1 for crosses, _, origin, _ in bits]
    after = [shifted(jnp.where(crosses, out, never)) == 1 for crosses, out, _, _ in bits]
    index = jnp.zeros((SUBLANES, LANES), jnp.int32)
    for b in range(LANE_BITS):
        index = index + lax.shift_left(lane >> b & 1, jnp.full((SUBLANES, LANES), lanes[b]))
    flips = [jnp.where(crosses, lax.shift_left(jnp.int32(1), origin), 0) for crosses, _, origin, _ in bits]
    targets = [lax.shift_left(jnp.int32(1), target) for _, _, _, target in bits]

    def trade(tiles, masks):
        for q in range(TILE_BITS):
            for at in range(TILES):
                if not at >> q & 1:
                    low, high = tiles[at], tiles[at + (1 << q)]
                    tiles[at] = jnp.where(masks[q], high, low)
                    tiles[at + (1 << q)] = jnp.where(masks[q], low, high)
        return tiles

    for part in range(2):
        tiles = trade([load(part, at) for at in range(TILES)], before)
        tiles = [
            jnp.take_along_axis(tiles[at], index ^ jnp.full((SUBLANES, LANES), combine(flips, at)), axis=1)
            for at in range(TILES)
        ]
        for at, tile in enumerate(trade(tiles, after)):
            store(part, combine(targets, at), tile)


def local_gates(plans, load, gates, scratch, out_ref, sublane_bit):
    def store(part, tile, value):
        scratch[part, tile] = value

    permute(load, store, plans)
    out = apply_rows(scratch[...].reshape(2 * TILES, SUBLANES, LANES), gates(0))
    tiles = jnp.concatenate(
        [out[:, :LANES].reshape(TILES, SUBLANES, LANES), out[:, LANES:].reshape(TILES, SUBLANES, LANES)], axis=0
    )
    tiles = apply_columns(tiles, gates(1))
    out = apply_rows(tiles, gates(2))
    for bit in range(2):
        piece = out[:, bit * LANES : (bit + 1) * LANES].reshape(2, TILES // 2, SUBLANES, LANES)
        for top, swapped in enumerate(swap_sublane_tile(piece[0], piece[1], sublane_bit)):
            for at in range(TILES // 2):
                out_ref[wire_place(top * TILES + 2 * at + bit)] = swapped[at]


def first_kernel(perm_hbm, state_hbm, gates_hbm, out_ref, perm_ref, state_ref, gates_ref, scratch, table, arrived):
    perm_copy = pltpu.make_async_copy(perm_hbm, perm_ref, arrived.at[4])
    perm_copy.start()
    copies = [pltpu.make_async_copy(state_hbm, state_ref, arrived.at[0])]
    for which in range(3):
        copies.append(pltpu.make_async_copy(gates_hbm.at[0, which], gates_ref.at[which], arrived.at[1 + which]))
    for copy in copies:
        copy.start()
    perm_copy.wait()
    plans = plan(perm_ref, 0, table)
    copies[0].wait()

    def load(part, tile):
        return state_ref[part, :, tile * LANES : (tile + 1) * LANES]

    def gates(which):
        copies[1 + which].wait()
        form = sending_gate if which == 2 else wide_gate
        return halves(form(gates_ref[which, 0], gates_ref[which, 1]))

    local_gates(plans, load, gates, scratch, out_ref, 1)


def gate_kernel(gates_ref, out_ref):
    ready = [
        middle_gate(gates_ref.at[0, 3]),
        wide_gate(gates_ref[1, 0, 0], gates_ref[1, 0, 1]),
        wide_gate(gates_ref[1, 1, 0], gates_ref[1, 1, 1]),
        sending_gate(gates_ref[1, 2, 0], gates_ref[1, 2, 1]),
        last_gate(gates_ref.at[1, 3]),
    ]
    for at, gate in enumerate(ready):
        out_ref[at, 0], out_ref[at, 1] = halves(gate)


def middle_kernel(perm_ref, tiles_ref, gates_ref, out_ref, before, scratch, table):
    plans = plan(perm_ref, 1, table)

    def gates(which):
        return gates_ref[1 + which, 0], gates_ref[1 + which, 1]

    before[...] = apply_columns(arrived_tiles(tiles_ref), gates(-1)).reshape(before.shape)

    def load(part, tile):
        return before[part, tile]

    local_gates(plans, load, gates, scratch, out_ref, 2)


def last_kernel(tiles_ref, gates_ref, out_ref):
    tiles = swap_sublane_lane(swap_sublane_lane(arrived_tiles(tiles_ref), 0, 5), 2, 6)
    columns = jnp.concatenate([tiles[:TILES].reshape(WIDE, LANES), tiles[TILES:].reshape(WIDE, LANES)], axis=1)
    out = product((gates_ref[4, 0], gates_ref[4, 1]), halves(columns), ((1,), (0,)))
    sides = [
        swap_sublane_lane(out[:, at : at + LANES].reshape(TILES, SUBLANES, LANES), 0, 5) for at in (0, LANES)
    ]
    for bit, side in enumerate(swap_sublane_tile(sides[0], sides[1], 1)):
        side = swap_sublane_lane(side, 2, 6)
        for at in range(TILES):
            part, tile = at // (TILES // 2), 2 * (at % (TILES // 2)) + bit
            out_ref[part, :, tile * LANES : (tile + 1) * LANES] = side[at]


SMEM = pl.BlockSpec(memory_space=pltpu.SMEM)
HBM = pl.BlockSpec(memory_space=pltpu.HBM)
VMEM = pl.BlockSpec(memory_space=pltpu.VMEM)
ALL_VMEM = pltpu.CompilerParams(vmem_limit_bytes=67043328)
PARAMS = pltpu.CompilerParams(vmem_limit_bytes=12 << 20)
TILE_SHAPE = (2 * TILES, SUBLANES, LANES)
SCRATCH = pltpu.VMEM((2, TILES, SUBLANES, LANES), jnp.float32)
READY = jax.ShapeDtypeStruct((5, 2, WIDE, WIDE), jnp.bfloat16)
TO_SEND = jax.ShapeDtypeStruct(TILE_SHAPE, jnp.float32)
DEV = ("z0", "z1", "z2", "z3", "dev_low")


def exchange(tiles, axes):
    ways = 1
    for axis in axes:
        ways *= lax.axis_size(axis)
    chunks = tiles.reshape(ways, -1, LANES)
    return lax.all_to_all(chunks, axes, split_axis=0, concat_axis=0, tiled=True).reshape(TILE_SHAPE)


def on_device(state, gates, local_perm):
    tiles = pl.pallas_call(
        first_kernel,
        out_shape=TO_SEND,
        in_specs=[HBM, HBM, HBM],
        out_specs=VMEM,
        scratch_shapes=[
            pltpu.SMEM(local_perm.shape, jnp.int32),
            pltpu.VMEM(state.shape, jnp.float32),
            pltpu.VMEM((3,) + gates.shape[2:], jnp.float32),
            SCRATCH,
            TABLE,
            pltpu.SemaphoreType.DMA((5,)),
        ],
        compiler_params=PARAMS,
    )(*(pltpu.with_memory_space_constraint(array, pltpu.HBM) for array in (local_perm, state, gates)))
    ready = pl.pallas_call(
        gate_kernel,
        out_shape=READY,
        in_specs=[VMEM],
        out_specs=VMEM,
        compiler_params=PARAMS,
        cost_estimate=pl.CostEstimate(flops=10**8, bytes_accessed=4 * 10**6, transcendentals=0),
    )(gates)
    tiles = exchange(tiles, DEV + ("grp1", "grp0"))
    tiles = pl.pallas_call(
        middle_kernel,
        out_shape=TO_SEND,
        in_specs=[SMEM, VMEM, VMEM],
        out_specs=VMEM,
        scratch_shapes=[SCRATCH, SCRATCH, TABLE],
        compiler_params=PARAMS,
    )(local_perm, tiles, ready)
    tiles = exchange(tiles, DEV + ("grp1",))
    return pl.pallas_call(
        last_kernel,
        out_shape=jax.ShapeDtypeStruct(state.shape, jnp.float32),
        in_specs=[VMEM, VMEM],
        out_specs=VMEM,
        compiler_params=PARAMS,
    )(tiles, ready)


def solution(mesh):
    groups, devs = mesh.devices.shape
    names = ("grp_rest", "grp1", "grp0", "z3", "z2", "z1", "z0", "dev_low")
    split = Mesh(mesh.devices.reshape(groups // 4, 2, 2, 2, 2, 2, 2, devs // 16), names)
    placed = P(None, None, names)
    return jax.shard_map(
        on_device,
        mesh=split,
        in_specs=(placed, P(), P()),
        out_specs=placed,
        check_vma=False,
    )
```

```python
import functools

import jax
import jax.numpy as jnp
from jax import lax
from jax.experimental import pallas as pl
from jax.experimental.pallas import tpu as pltpu
from jax.sharding import Mesh, PartitionSpec as P

CYCLES = 2
LANE_BITS = 7
TILE_BITS = 5
TILES = 1 << TILE_BITS
SUBLANES = 8
LANES = 1 << LANE_BITS
WIDE = 2 * LANES


def lane_iota(shape):
    return lax.broadcasted_iota(jnp.int32, shape, len(shape) - 1)


def sublane_iota(shape):
    return lax.broadcasted_iota(jnp.int32, shape, len(shape) - 2)


def halves(array):
    high = array.astype(jnp.bfloat16)
    return high, (array - high.astype(jnp.float32)).astype(jnp.bfloat16)


def product(left, right):
    dims = (((1,), (1,)), ((), ()))
    dot = functools.partial(lax.dot_general, dimension_numbers=dims, preferred_element_type=jnp.float32)
    return dot(left[0], right[0]) + (dot(left[0], right[1]) + dot(left[1], right[0]))


def by_rows(left, right):
    cut = WIDE // 2
    return jnp.concatenate(
        [product(tuple(half[at : at + cut] for half in left), right) for at in (0, cut)], axis=0
    )


def by_columns(left, right):
    cut = WIDE // 2
    return jnp.concatenate(
        [product(left, tuple(half[at : at + cut] for half in right)) for at in (0, cut)], axis=1
    )


def set_lanes(lane_bit):
    return lane_iota((SUBLANES, LANES)) >> lane_bit & 1 == 1


def trade(tiles, masks):
    tiles = list(tiles)
    for tile_bit, mask in masks:
        for at in range(len(tiles)):
            if not at >> tile_bit & 1:
                low, high = tiles[at], tiles[at + (1 << tile_bit)]
                tiles[at] = jnp.where(mask, high, low)
                tiles[at + (1 << tile_bit)] = jnp.where(mask, low, high)
    return tiles


def exchange_tile_lane(tiles, pairs):
    masks = [(tile_bit, set_lanes(lane_bit)) for tile_bit, lane_bit in pairs]
    lane = lane_iota((SUBLANES, LANES))
    tiles = trade(tiles, masks)
    for at in range(len(tiles)):
        hop = sum((at >> tile_bit & 1) << lane_bit for tile_bit, lane_bit in pairs)
        if 2 * hop == LANES:
            tiles[at] = pltpu.roll(tiles[at], hop, 1)
        elif hop:
            tiles[at] = jnp.take_along_axis(tiles[at], lane ^ hop, axis=1)
    return trade(tiles, masks)


def exchange_tile_sublane(tiles, tile_bit, sublane_bit):
    tiles = list(tiles)
    step = 1 << sublane_bit
    clear = sublane_iota((SUBLANES, LANES)) >> sublane_bit & 1 == 0
    for at in range(len(tiles)):
        if not at >> tile_bit & 1:
            low, high = tiles[at], tiles[at + (1 << tile_bit)]
            tiles[at] = jnp.where(clear, low, pltpu.roll(high, step, 0))
            tiles[at + (1 << tile_bit)] = jnp.where(clear, pltpu.roll(low, SUBLANES - step, 0), high)
    return tiles


def tiles_of(array, column):
    return [
        array[at * SUBLANES : (at + 1) * SUBLANES, column * LANES : (column + 1) * LANES] for at in range(TILES)
    ]


def matrix_of(left, right):
    return halves(jnp.concatenate([jnp.concatenate(left, axis=0), jnp.concatenate(right, axis=0)], axis=1))


def wide_gate(real, imag):
    return jnp.concatenate(
        [jnp.concatenate([real, -imag], axis=1), jnp.concatenate([imag, real], axis=1)], axis=0
    )


def sending_gate(real, imag):
    gate = wide_gate(real, imag)
    cut = LANES // 2
    return jnp.concatenate([gate[at : at + cut] for at in (0, LANES, cut, LANES + cut)], axis=0)


def turned(ref):
    return jnp.concatenate([ref[pl.ds(low, LANES // 4, stride=4)] for low in range(4)], axis=0)


def take_lanes(array, index):
    rows = [
        jnp.take_along_axis(array[r : r + SUBLANES], index, axis=1) for r in range(0, array.shape[0], SUBLANES)
    ]
    return jnp.concatenate(rows, axis=0)


def receiving_gate(real, imag):
    lane = lane_iota((SUBLANES, LANES))
    part = lane_iota((1, LANES)) >> LANE_BITS - 1 & 1
    blocks = []
    for half in range(2):
        index = half * (LANES // 2) + ((lane & TILES - 1) << 1) + (lane >> TILE_BITS & 1)
        real_half, imag_half = take_lanes(real, index), take_lanes(imag, index)
        blocks.append(
            jnp.concatenate(
                [jnp.where(part == 0, real_half, -imag_half), jnp.where(part == 0, imag_half, real_half)], axis=0
            )
        )
    return jnp.concatenate(blocks, axis=1)


def wire_place(tile):
    z, low = tile >> 2, tile & 3
    return (z & 1) << 5 | (z >> 1 & 1) << 4 | (z >> 2 & 1) << 3 | (z >> 3 & 1) << 2 | low


def arrived_tiles(tiles_ref):
    return [tiles_ref[wire_place(tile)] for tile in range(2 * TILES)]


OUT_OF = 0
CROSSING = OUT_OF + LANE_BITS + TILE_BITS
LANE_OF = CROSSING + TILE_BITS + 1
TABLE = pltpu.SMEM((LANE_OF + LANE_BITS + TILE_BITS,), jnp.int32)


def plan(source_of, table):
    source = [source_of(b) for b in range(LANE_BITS + TILE_BITS)]
    for b in range(LANE_BITS + TILE_BITS):
        table[OUT_OF + source[b]] = jnp.int32(b)
    count = jnp.int32(0)
    for b in range(LANE_BITS, LANE_BITS + TILE_BITS):
        table[CROSSING + count] = jnp.int32(b)
        count = count + jnp.where(source[b] < LANE_BITS, 1, 0)
    for b in range(LANE_BITS):
        table[LANE_OF + b] = jnp.int32(b)
    rank = jnp.int32(0)
    bits = []
    for q in range(TILE_BITS):
        out = table[OUT_OF + LANE_BITS + q]
        crosses = out < LANE_BITS
        partner = table[CROSSING + jnp.where(crosses, rank, 0)]
        rank = rank + jnp.where(crosses, 1, 0)
        origin = source_of(partner)
        table[LANE_OF + LANE_BITS + q] = origin
        target = jnp.where(crosses, partner, out) - LANE_BITS
        target = jnp.where(target == 0, TILE_BITS - 1, target - 1)
        bits.append((crosses, out, origin, target))
    lanes = [table[LANE_OF + source[b]] for b in range(LANE_BITS)]
    return bits, lanes


def combine(basis, value):
    total = jnp.int32(0)
    for bit in range(TILE_BITS):
        if value >> bit & 1:
            total = total + basis[bit]
    return total


def permute(load, store, plans):
    bits, lanes = plans
    lane = lane_iota((SUBLANES, LANES))

    def shifted(amount):
        return lax.shift_right_logical(lane, jnp.full((SUBLANES, LANES), amount)) & 1

    never = 31
    before = [(q, shifted(jnp.where(bit[0], bit[2], never)) == 1) for q, bit in enumerate(bits)]
    after = [(q, shifted(jnp.where(bit[0], bit[1], never)) == 1) for q, bit in enumerate(bits)]
    index = jnp.zeros((SUBLANES, LANES), jnp.int32)
    for b in range(LANE_BITS):
        index = index + lax.shift_left(lane >> b & 1, jnp.full((SUBLANES, LANES), lanes[b]))
    flips = [jnp.where(crosses, lax.shift_left(jnp.int32(1), origin), 0) for crosses, _, origin, _ in bits]
    targets = [lax.shift_left(jnp.int32(1), target) for _, _, _, target in bits]
    for part in range(2):
        tiles = trade([load(part, at) for at in range(TILES)], before)
        tiles = [
            jnp.take_along_axis(tiles[at], index ^ jnp.full((SUBLANES, LANES), combine(flips, at)), axis=1)
            for at in range(TILES)
        ]
        for at, tile in enumerate(trade(tiles, after)):
            store(part, combine(targets, at), tile)


def local_gates(plans, load, gates, scratch, out_ref, partners, top, last_product):
    def store(part, tile, value):
        scratch[part, tile] = value

    permute(load, store, plans)
    parts = scratch[...].reshape(2, TILES * SUBLANES, LANES)
    out = by_rows(gates(0), halves(jnp.concatenate([parts[0], parts[1]], axis=1)))
    sides = []
    for part in range(2):
        rows = slice(part * (TILES // 2), (part + 1) * (TILES // 2))
        sides.append(exchange_tile_lane(tiles_of(out, 0)[rows] + tiles_of(out, 1)[rows], ((4, 2), (3, 1), (2, 0))))
    out = by_rows(gates(1), matrix_of(*sides))
    sides = []
    for part in range(2):
        rows = slice(part * (TILES // 2), (part + 1) * (TILES // 2))
        sides.append(exchange_tile_lane(tiles_of(out, 0)[rows] + tiles_of(out, 1)[rows], ((3, 6), (2, 5))))
    out = last_product(matrix_of(*sides), gates(2))
    names = ["h3", "h4", "t0", "t1", "t2"]
    for sublane_bit, tile_bit in enumerate(partners):
        names[tile_bit] = ("h0", "h1", "h2")[sublane_bit]
    order = ("h0", "h1", "h2", "h3")
    for low in range(2):
        tiles = tiles_of(out, low)
        for sublane_bit, tile_bit in enumerate(partners):
            tiles = exchange_tile_sublane(tiles, tile_bit, sublane_bit)
        for at, tile in enumerate(tiles):
            device = (at >> top & 1) << 5 | low
            for place, name in enumerate(order):
                device |= (at >> names.index(name) & 1) << place + 1
            out_ref[wire_place(device)] = tile


def first_kernel(perm_hbm, state_hbm, gates_hbm, out_ref, perm_ref, state_ref, gates_ref, scratch, table, arrived):
    perm_copy = pltpu.make_async_copy(perm_hbm, perm_ref, arrived.at[4])
    perm_copy.start()
    copies = [pltpu.make_async_copy(state_hbm, state_ref, arrived.at[0])]
    for which in range(3):
        copies.append(pltpu.make_async_copy(gates_hbm.at[0, which], gates_ref.at[which], arrived.at[1 + which]))
    for copy in copies:
        copy.start()
    perm_copy.wait()
    plans = plan(lambda b: perm_ref[0, b], table)
    copies[0].wait()

    def load(part, tile):
        return state_ref[part, :, tile * LANES : (tile + 1) * LANES]

    def gates(which):
        copies[1 + which].wait()
        if which == 1:
            return halves(wide_gate(turned(gates_ref.at[which, 0]), turned(gates_ref.at[which, 1])))
        form = sending_gate if which == 2 else wide_gate
        return halves(form(gates_ref[which, 0], gates_ref[which, 1]))

    local_gates(plans, load, gates, scratch, out_ref, (2, 1, 4), 3, by_rows)


def gate_kernel(gates_ref, out_ref):
    ready = [
        receiving_gate(gates_ref[0, 3, 0], gates_ref[0, 3, 1]),
        wide_gate(gates_ref[1, 0, 0], gates_ref[1, 0, 1]),
        wide_gate(turned(gates_ref.at[1, 1, 0]), turned(gates_ref.at[1, 1, 1])),
        sending_gate(gates_ref[1, 2, 0], gates_ref[1, 2, 1]),
        receiving_gate(turned(gates_ref.at[1, 3, 0]), turned(gates_ref.at[1, 3, 1])),
    ]
    for at, gate in enumerate(ready):
        out_ref[at, 0], out_ref[at, 1] = halves(gate)


LOW_FIVE = tuple((bit, bit) for bit in range(TILE_BITS))


def middle_kernel(perm_ref, tiles_ref, gates_ref, out_ref, scratch, table):
    def source_of(b):
        source = perm_ref[1, b]
        return jnp.where(source >= TILE_BITS, source - TILE_BITS, source + LANE_BITS)

    plans = plan(source_of, table)

    def gates(which):
        return gates_ref[1 + which, 0], gates_ref[1 + which, 1]

    tiles = arrived_tiles(tiles_ref)
    out = by_columns(
        matrix_of(exchange_tile_lane(tiles[:TILES], LOW_FIVE), exchange_tile_lane(tiles[TILES:], LOW_FIVE)), gates(-1)
    )
    before = (tiles_of(out, 0), tiles_of(out, 1))

    def load(part, tile):
        return before[part][tile]

    local_gates(plans, load, gates, scratch, out_ref, (2, 3, 1), 4, by_columns)


def last_kernel(tiles_ref, gates_ref, out_ref):
    tiles = exchange_tile_sublane(arrived_tiles(tiles_ref), TILE_BITS, 1)
    out = by_columns(
        matrix_of(exchange_tile_lane(tiles[:TILES], LOW_FIVE), exchange_tile_lane(tiles[TILES:], LOW_FIVE)),
        (gates_ref[4, 0], gates_ref[4, 1]),
    )
    for part in range(2):
        for at, tile in enumerate(exchange_tile_lane(tiles_of(out, part), LOW_FIVE)):
            out_ref[part, :, at * LANES : (at + 1) * LANES] = tile


SMEM = pl.BlockSpec(memory_space=pltpu.SMEM)
HBM = pl.BlockSpec(memory_space=pltpu.HBM)
VMEM = pl.BlockSpec(memory_space=pltpu.VMEM)
ALL_VMEM = pltpu.CompilerParams(vmem_limit_bytes=67043328)
PARAMS = pltpu.CompilerParams(vmem_limit_bytes=12 << 20)
TILE_SHAPE = (2 * TILES, SUBLANES, LANES)
SCRATCH = pltpu.VMEM((2, TILES, SUBLANES, LANES), jnp.float32)
READY = jax.ShapeDtypeStruct((5, 2, WIDE, WIDE), jnp.bfloat16)
TO_SEND = jax.ShapeDtypeStruct(TILE_SHAPE, jnp.float32)
DEV = ("z0", "z1", "z2", "z3", "dev_low")


def exchange(tiles, axes):
    ways = 1
    for axis in axes:
        ways *= lax.axis_size(axis)
    chunks = tiles.reshape(ways, -1, LANES)
    return lax.all_to_all(chunks, axes, split_axis=0, concat_axis=0, tiled=True).reshape(TILE_SHAPE)


def on_device(state, gates, local_perm):
    tiles = pl.pallas_call(
        first_kernel,
        out_shape=TO_SEND,
        in_specs=[HBM, HBM, HBM],
        out_specs=VMEM,
        scratch_shapes=[
            pltpu.SMEM(local_perm.shape, jnp.int32),
            pltpu.VMEM(state.shape, jnp.float32),
            pltpu.VMEM((3,) + gates.shape[2:], jnp.float32),
            SCRATCH,
            TABLE,
            pltpu.SemaphoreType.DMA((5,)),
        ],
        compiler_params=PARAMS,
    )(*(pltpu.with_memory_space_constraint(array, pltpu.HBM) for array in (local_perm, state, gates)))
    ready = pl.pallas_call(
        gate_kernel,
        out_shape=READY,
        in_specs=[VMEM],
        out_specs=VMEM,
        compiler_params=PARAMS,
        cost_estimate=pl.CostEstimate(flops=10**8, bytes_accessed=4 * 10**6, transcendentals=0),
    )(gates)
    tiles = exchange(tiles, DEV + ("grp1", "grp0"))
    tiles = pl.pallas_call(
        middle_kernel,
        out_shape=TO_SEND,
        in_specs=[SMEM, VMEM, VMEM],
        out_specs=VMEM,
        scratch_shapes=[SCRATCH, TABLE],
        compiler_params=PARAMS,
    )(local_perm, tiles, ready)
    tiles = exchange(tiles, DEV + ("grp1",))
    return pl.pallas_call(
        last_kernel,
        out_shape=jax.ShapeDtypeStruct(state.shape, jnp.float32),
        in_specs=[VMEM, VMEM],
        out_specs=VMEM,
        compiler_params=PARAMS,
    )(tiles, ready)


def solution(mesh):
    groups, devs = mesh.devices.shape
    names = ("grp_rest", "grp1", "grp0", "z3", "z2", "z1", "z0", "dev_low")
    split = Mesh(mesh.devices.reshape(groups // 4, 2, 2, 2, 2, 2, 2, devs // 16), names)
    placed = P(None, None, names)
    return jax.shard_map(
        on_device,
        mesh=split,
        in_specs=(placed, P(), P()),
        out_specs=placed,
        check_vma=False,
    )
```

```python
import functools

import jax
import jax.numpy as jnp
from jax import lax
from jax.experimental import pallas as pl
from jax.experimental.pallas import tpu as pltpu
from jax.sharding import Mesh, PartitionSpec as P

CYCLES = 2
LANE_BITS = 7
TILE_BITS = 5
TILES = 1 << TILE_BITS
SUBLANES = 8
LANES = 1 << LANE_BITS
WIDE = 2 * LANES


def lane_iota(shape):
    return lax.broadcasted_iota(jnp.int32, shape, len(shape) - 1)


def sublane_iota(shape):
    return lax.broadcasted_iota(jnp.int32, shape, len(shape) - 2)


def halves(array):
    high = array.astype(jnp.bfloat16)
    return high, (array - high.astype(jnp.float32)).astype(jnp.bfloat16)


def product(left, right, right_axis=1):
    dims = (((1,), (right_axis,)), ((), ()))
    dot = functools.partial(lax.dot_general, dimension_numbers=dims, preferred_element_type=jnp.float32)
    return dot(left[0], right[0]) + (dot(left[0], right[1]) + dot(left[1], right[0]))


def by_rows(left, right):
    cut = WIDE // 2
    return jnp.concatenate(
        [product(tuple(half[at : at + cut] for half in left), right) for at in (0, cut)], axis=0
    )


def by_columns(left, right):
    cut = WIDE // 2
    return jnp.concatenate(
        [product(left, tuple(half[at : at + cut] for half in right)) for at in (0, cut)], axis=1
    )


def set_lanes(lane_bit):
    return lane_iota((SUBLANES, LANES)) >> lane_bit & 1 == 1


def trade(tiles, masks):
    tiles = list(tiles)
    for tile_bit, mask in masks:
        for at in range(len(tiles)):
            if not at >> tile_bit & 1:
                low, high = tiles[at], tiles[at + (1 << tile_bit)]
                tiles[at] = jnp.where(mask, high, low)
                tiles[at + (1 << tile_bit)] = jnp.where(mask, low, high)
    return tiles


def exchange_tile_lane(tiles, pairs):
    masks = [(tile_bit, set_lanes(lane_bit)) for tile_bit, lane_bit in pairs]
    lane = lane_iota((SUBLANES, LANES))
    tiles = trade(tiles, masks)
    for at in range(len(tiles)):
        hop = sum((at >> tile_bit & 1) << lane_bit for tile_bit, lane_bit in pairs)
        if 2 * hop == LANES:
            tiles[at] = pltpu.roll(tiles[at], hop, 1)
        elif hop:
            tiles[at] = jnp.take_along_axis(tiles[at], lane ^ hop, axis=1)
    return trade(tiles, masks)


def exchange_tile_sublane(tiles, tile_bit, sublane_bit):
    tiles = list(tiles)
    step = 1 << sublane_bit
    clear = sublane_iota((SUBLANES, LANES)) >> sublane_bit & 1 == 0
    for at in range(len(tiles)):
        if not at >> tile_bit & 1:
            low, high = tiles[at], tiles[at + (1 << tile_bit)]
            tiles[at] = jnp.where(clear, low, pltpu.roll(high, step, 0))
            tiles[at + (1 << tile_bit)] = jnp.where(clear, pltpu.roll(low, SUBLANES - step, 0), high)
    return tiles


def tiles_of(array, column):
    return [
        array[at * SUBLANES : (at + 1) * SUBLANES, column * LANES : (column + 1) * LANES] for at in range(TILES)
    ]


def matrix_of(left, right):
    return halves(jnp.concatenate([jnp.concatenate(left, axis=0), jnp.concatenate(right, axis=0)], axis=1))


def flip_lane_bit(tiles, lane_bit):
    hop = 1 << lane_bit
    if 2 * hop == LANES:
        return pltpu.roll(tiles, hop, 2)
    index = lane_iota((SUBLANES, LANES)) ^ hop
    return jnp.stack([jnp.take_along_axis(tiles[at], index, axis=1) for at in range(tiles.shape[0])])


def swap_sublane_lane(tiles, sublane_bit, lane_bit):
    step = 1 << sublane_bit
    one_tile = (1, SUBLANES, LANES)
    in_sublane = sublane_iota(one_tile) >> sublane_bit & 1
    in_lane = lane_iota(one_tile) >> lane_bit & 1
    if 2 * step == SUBLANES:
        flipped = pltpu.roll(tiles, step, 1)
    else:
        flipped = jnp.where(in_sublane == 0, pltpu.roll(tiles, SUBLANES - step, 1), pltpu.roll(tiles, step, 1))
    return jnp.where(in_sublane == in_lane, tiles, flip_lane_bit(flipped, lane_bit))


def swap_sublane_tile(low, high, sublane_bit):
    step = 1 << sublane_bit
    clear = sublane_iota((1, SUBLANES, LANES)) >> sublane_bit & 1 == 0
    new_low = jnp.where(clear, low, pltpu.roll(high, step, 1))
    new_high = jnp.where(clear, pltpu.roll(low, SUBLANES - step, 1), high)
    return new_low, new_high


def swap_middle_rows(array):
    tiles = array.reshape(-1, SUBLANES, LANES)
    row = sublane_iota((1, SUBLANES, LANES)) >> 1 & 3
    tiles = jnp.where(
        row == 1, pltpu.roll(tiles, SUBLANES - 2, 1), jnp.where(row == 2, pltpu.roll(tiles, 2, 1), tiles)
    )
    return tiles.reshape(array.shape)


def wide_gate(real, imag):
    return jnp.concatenate(
        [jnp.concatenate([real, -imag], axis=1), jnp.concatenate([imag, real], axis=1)], axis=0
    )


def sending_gate(real, imag):
    gate = wide_gate(real, imag)
    cut = LANES // 2
    return jnp.concatenate([gate[at : at + cut] for at in (0, LANES, cut, LANES + cut)], axis=0)


def turned(ref):
    return jnp.concatenate([ref[pl.ds(low, LANES // 4, stride=4)] for low in range(4)], axis=0)


def take_lanes(array, index):
    rows = [
        jnp.take_along_axis(array[r : r + SUBLANES], index, axis=1) for r in range(0, array.shape[0], SUBLANES)
    ]
    return jnp.concatenate(rows, axis=0)


def receiving_gate(real, imag):
    lane = lane_iota((SUBLANES, LANES))
    part = lane_iota((1, LANES)) >> LANE_BITS - 1 & 1
    blocks = []
    for half in range(2):
        index = half * (LANES // 2) + ((lane & TILES - 1) << 1) + (lane >> TILE_BITS & 1)
        real_half, imag_half = take_lanes(real, index), take_lanes(imag, index)
        blocks.append(
            jnp.concatenate(
                [jnp.where(part == 0, real_half, -imag_half), jnp.where(part == 0, imag_half, real_half)], axis=0
            )
        )
    return jnp.concatenate(blocks, axis=1)


def last_gate(real, imag):
    real, imag = swap_middle_rows(real), swap_middle_rows(imag)
    lane = lane_iota((SUBLANES, LANES))
    part = lane_iota((1, LANES)) >> 2 & 1
    blocks = []
    for half in range(2):
        index = ((lane >> 1 & 1) << 6) + half * (LANES // 4) + ((lane >> 3) << 1) + (lane & 1)
        real_half, imag_half = take_lanes(real, index), take_lanes(imag, index)
        blocks.append(
            jnp.concatenate(
                [jnp.where(part == 0, real_half, -imag_half), jnp.where(part == 0, imag_half, real_half)], axis=0
            )
        )
    return jnp.concatenate(blocks, axis=1)


def wire_place(tile):
    z, low = tile >> 2, tile & 3
    return (z & 1) << 5 | (z >> 1 & 1) << 4 | (z >> 2 & 1) << 3 | (z >> 3 & 1) << 2 | low


def arrived_tiles(tiles_ref):
    return [tiles_ref[wire_place(tile)] for tile in range(2 * TILES)]


OUT_OF = 0
CROSSING = OUT_OF + LANE_BITS + TILE_BITS
LANE_OF = CROSSING + TILE_BITS + 1
TABLE = pltpu.SMEM((LANE_OF + LANE_BITS + TILE_BITS,), jnp.int32)


def plan(source_of, table):
    source = [source_of(b) for b in range(LANE_BITS + TILE_BITS)]
    for b in range(LANE_BITS + TILE_BITS):
        table[OUT_OF + source[b]] = jnp.int32(b)
    count = jnp.int32(0)
    for b in range(LANE_BITS, LANE_BITS + TILE_BITS):
        table[CROSSING + count] = jnp.int32(b)
        count = count + jnp.where(source[b] < LANE_BITS, 1, 0)
    for b in range(LANE_BITS):
        table[LANE_OF + b] = jnp.int32(b)
    rank = jnp.int32(0)
    bits = []
    for q in range(TILE_BITS):
        out = table[OUT_OF + LANE_BITS + q]
        crosses = out < LANE_BITS
        partner = table[CROSSING + jnp.where(crosses, rank, 0)]
        rank = rank + jnp.where(crosses, 1, 0)
        origin = source_of(partner)
        table[LANE_OF + LANE_BITS + q] = origin
        target = jnp.where(crosses, partner, out) - LANE_BITS
        target = jnp.where(target == 0, TILE_BITS - 1, target - 1)
        bits.append((crosses, out, origin, target))
    lanes = [table[LANE_OF + source[b]] for b in range(LANE_BITS)]
    return bits, lanes


def combine(basis, value):
    total = jnp.int32(0)
    for bit in range(TILE_BITS):
        if value >> bit & 1:
            total = total + basis[bit]
    return total


def permute(load, store, plans):
    bits, lanes = plans
    lane = lane_iota((SUBLANES, LANES))

    def shifted(amount):
        return lax.shift_right_logical(lane, jnp.full((SUBLANES, LANES), amount)) & 1

    never = 31
    before = [(q, shifted(jnp.where(bit[0], bit[2], never)) == 1) for q, bit in enumerate(bits)]
    after = [(q, shifted(jnp.where(bit[0], bit[1], never)) == 1) for q, bit in enumerate(bits)]
    index = jnp.zeros((SUBLANES, LANES), jnp.int32)
    for b in range(LANE_BITS):
        index = index + lax.shift_left(lane >> b & 1, jnp.full((SUBLANES, LANES), lanes[b]))
    flips = [jnp.where(crosses, lax.shift_left(jnp.int32(1), origin), 0) for crosses, _, origin, _ in bits]
    targets = [lax.shift_left(jnp.int32(1), target) for _, _, _, target in bits]
    for part in range(2):
        tiles = trade([load(part, at) for at in range(TILES)], before)
        tiles = [
            jnp.take_along_axis(tiles[at], index ^ jnp.full((SUBLANES, LANES), combine(flips, at)), axis=1)
            for at in range(TILES)
        ]
        for at, tile in enumerate(trade(tiles, after)):
            store(part, combine(targets, at), tile)


def local_gates(plans, load, gates, scratch, out_ref, partners, top, last_product):
    def store(part, tile, value):
        scratch[part, tile] = value

    permute(load, store, plans)
    parts = scratch[...].reshape(2, TILES * SUBLANES, LANES)
    out = product(gates(0), halves(jnp.concatenate([parts[0], parts[1]], axis=1)))
    sides = []
    for part in range(2):
        rows = slice(part * (TILES // 2), (part + 1) * (TILES // 2))
        sides.append(exchange_tile_lane(tiles_of(out, 0)[rows] + tiles_of(out, 1)[rows], ((4, 2), (3, 1), (2, 0))))
    out = product(gates(1), matrix_of(*sides))
    sides = []
    for part in range(2):
        rows = slice(part * (TILES // 2), (part + 1) * (TILES // 2))
        sides.append(exchange_tile_lane(tiles_of(out, 0)[rows] + tiles_of(out, 1)[rows], ((3, 6), (2, 5))))
    out = last_product(matrix_of(*sides), gates(2))
    names = ["h3", "h4", "t0", "t1", "t2"]
    for sublane_bit, tile_bit in enumerate(partners):
        names[tile_bit] = ("h0", "h1", "h2")[sublane_bit]
    order = ("h0", "h1", "h2", "h3")
    for low in range(2):
        tiles = tiles_of(out, low)
        for sublane_bit, tile_bit in enumerate(partners):
            tiles = exchange_tile_sublane(tiles, tile_bit, sublane_bit)
        for at, tile in enumerate(tiles):
            device = (at >> top & 1) << 5 | low
            for place, name in enumerate(order):
                device |= (at >> names.index(name) & 1) << place + 1
            out_ref[wire_place(device)] = tile


def first_kernel(perm_hbm, state_hbm, gates_hbm, out_ref, perm_ref, state_ref, gates_ref, scratch, table, arrived):
    perm_copy = pltpu.make_async_copy(perm_hbm, perm_ref, arrived.at[4])
    perm_copy.start()
    copies = [pltpu.make_async_copy(state_hbm, state_ref, arrived.at[0])]
    for which in range(3):
        copies.append(pltpu.make_async_copy(gates_hbm.at[0, which], gates_ref.at[which], arrived.at[1 + which]))
    for copy in copies:
        copy.start()
    perm_copy.wait()
    plans = plan(lambda b: perm_ref[0, b], table)
    copies[0].wait()

    def load(part, tile):
        return state_ref[part, :, tile * LANES : (tile + 1) * LANES]

    def gates(which):
        copies[1 + which].wait()
        if which == 1:
            return halves(wide_gate(turned(gates_ref.at[which, 0]), turned(gates_ref.at[which, 1])))
        form = sending_gate if which == 2 else wide_gate
        return halves(form(gates_ref[which, 0], gates_ref[which, 1]))

    local_gates(plans, load, gates, scratch, out_ref, (2, 1, 4), 3, product)


def gate_kernel(gates_hbm, out_ref, gates_ref, arrived):
    copy = pltpu.make_async_copy(gates_hbm, gates_ref, arrived)
    copy.start()
    copy.wait()
    ready = [
        receiving_gate(gates_ref[0, 3, 0], gates_ref[0, 3, 1]),
        wide_gate(gates_ref[1, 0, 0], gates_ref[1, 0, 1]),
        wide_gate(turned(gates_ref.at[1, 1, 0]), turned(gates_ref.at[1, 1, 1])),
        sending_gate(gates_ref[1, 2, 0], gates_ref[1, 2, 1]),
        last_gate(gates_ref[1, 3, 0], gates_ref[1, 3, 1]),
    ]
    for at, gate in enumerate(ready):
        out_ref[at, 0], out_ref[at, 1] = halves(gate)


LOW_FIVE = tuple((bit, bit) for bit in range(TILE_BITS))


def middle_kernel(perm_ref, tiles_ref, gates_ref, out_ref, scratch, table):
    def source_of(b):
        source = perm_ref[1, b]
        return jnp.where(source >= TILE_BITS, source - TILE_BITS, source + LANE_BITS)

    plans = plan(source_of, table)

    def gates(which):
        return gates_ref[1 + which, 0], gates_ref[1 + which, 1]

    tiles = arrived_tiles(tiles_ref)
    out = product(
        matrix_of(exchange_tile_lane(tiles[:TILES], LOW_FIVE), exchange_tile_lane(tiles[TILES:], LOW_FIVE)), gates(-1)
    )
    before = (tiles_of(out, 0), tiles_of(out, 1))

    def load(part, tile):
        return before[part][tile]

    local_gates(plans, load, gates, scratch, out_ref, (2, 3, 1), 4, product)


def last_kernel(tiles_ref, gates_ref, out_ref):
    tiles = swap_sublane_lane(swap_sublane_lane(jnp.stack(arrived_tiles(tiles_ref)), 0, 5), 2, 6)
    columns = jnp.concatenate([tiles[:TILES].reshape(WIDE, LANES), tiles[TILES:].reshape(WIDE, LANES)], axis=1)
    out = product((gates_ref[4, 0], gates_ref[4, 1]), halves(columns), 0)
    sides = [
        swap_sublane_lane(out[:, at : at + LANES].reshape(TILES, SUBLANES, LANES), 0, 5) for at in (0, LANES)
    ]
    for bit, side in enumerate(swap_sublane_tile(sides[0], sides[1], 1)):
        side = swap_sublane_lane(side, 2, 6)
        for at in range(TILES):
            part, tile = at // (TILES // 2), 2 * (at % (TILES // 2)) + bit
            out_ref[part, :, tile * LANES : (tile + 1) * LANES] = side[at]


SMEM = pl.BlockSpec(memory_space=pltpu.SMEM)
HBM = pl.BlockSpec(memory_space=pltpu.HBM)
VMEM = pl.BlockSpec(memory_space=pltpu.VMEM)
ALL_VMEM = pltpu.CompilerParams(vmem_limit_bytes=67043328)
PARAMS = pltpu.CompilerParams(vmem_limit_bytes=12 << 20)
TILE_SHAPE = (2 * TILES, SUBLANES, LANES)
SCRATCH = pltpu.VMEM((2, TILES, SUBLANES, LANES), jnp.float32)
READY = jax.ShapeDtypeStruct((5, 2, WIDE, WIDE), jnp.bfloat16)
TO_SEND = jax.ShapeDtypeStruct(TILE_SHAPE, jnp.float32)
DEV = ("z0", "z1", "z2", "z3", "dev_low")


def exchange(tiles, axes):
    ways = 1
    for axis in axes:
        ways *= lax.axis_size(axis)
    chunks = tiles.reshape(ways, -1, LANES)
    return lax.all_to_all(chunks, axes, split_axis=0, concat_axis=0, tiled=True).reshape(TILE_SHAPE)


def on_device(state, gates, local_perm):
    tiles = pl.pallas_call(
        first_kernel,
        out_shape=TO_SEND,
        in_specs=[HBM, HBM, HBM],
        out_specs=VMEM,
        scratch_shapes=[
            pltpu.SMEM(local_perm.shape, jnp.int32),
            pltpu.VMEM(state.shape, jnp.float32),
            pltpu.VMEM((3,) + gates.shape[2:], jnp.float32),
            SCRATCH,
            TABLE,
            pltpu.SemaphoreType.DMA((5,)),
        ],
        compiler_params=PARAMS,
    )(*(pltpu.with_memory_space_constraint(array, pltpu.HBM) for array in (local_perm, state, gates)))
    ready = pl.pallas_call(
        gate_kernel,
        out_shape=READY,
        in_specs=[HBM],
        out_specs=VMEM,
        scratch_shapes=[pltpu.VMEM(gates.shape, jnp.float32), pltpu.SemaphoreType.DMA],
        compiler_params=PARAMS,
        cost_estimate=pl.CostEstimate(flops=10**8, bytes_accessed=4 * 10**6, transcendentals=0),
    )(pltpu.with_memory_space_constraint(gates, pltpu.HBM))
    tiles = exchange(tiles, DEV + ("grp1", "grp0"))
    tiles = pl.pallas_call(
        middle_kernel,
        out_shape=TO_SEND,
        in_specs=[SMEM, VMEM, VMEM],
        out_specs=VMEM,
        scratch_shapes=[SCRATCH, TABLE],
        compiler_params=PARAMS,
    )(local_perm, tiles, ready)
    tiles = exchange(tiles, DEV + ("grp1",))
    return pl.pallas_call(
        last_kernel,
        out_shape=jax.ShapeDtypeStruct(state.shape, jnp.float32),
        in_specs=[VMEM, VMEM],
        out_specs=VMEM,
        compiler_params=PARAMS,
    )(tiles, ready)


def solution(mesh):
    groups, devs = mesh.devices.shape
    names = ("grp_rest", "grp1", "grp0", "z3", "z2", "z1", "z0", "dev_low")
    split = Mesh(mesh.devices.reshape(groups // 4, 2, 2, 2, 2, 2, 2, devs // 16), names)
    placed = P(None, None, names)
    return jax.shard_map(
        on_device,
        mesh=split,
        in_specs=(placed, P(), P()),
        out_specs=placed,
        check_vma=False,
    )
```
